32 devices in a mesh: ctx: 4 (over z), tp: 8 (over y, x, core).
Axes of the slice: x: 2, y: 2, z: 4, core: 2. Of those that a mesh axis runs over, the one named last changes fastest.
Arguments:
- q_nope: bfloat16 [512, 16384], P('ctx', 'tp'), may hold values from -5 to 5
- q_rope: bfloat16 [512, 8192], P('ctx', 'tp'), may hold values from -128 to 128
- cache_latent: bfloat16 [128, 576], P('ctx'), may hold values from -4 to 4
- group_latent: bfloat16 [512, 576], P('ctx'), may hold values from -4 to 4
- offset: int32 [1], replicated, may hold values from 128 to 255
- counts: int32 [4], replicated, may hold values from 1 to 32, as said below
- up_key: bfloat16 [128, 128, 512], P('tp'), may hold values from -0.5 to 0.5
- up_value: bfloat16 [128, 512, 128], P('tp'), may hold values from -0.25 to 0.25
- out_weight: bfloat16 [16384, 7168], P('tp'), may hold values from -0.0625 to 0.0625
Outputs:
- attn_out: bfloat16 [512, 7168], P('ctx', 'tp')
The draws below stay inside these ranges and needn't reach their ends.
Inputs may be any that keep to these rules, and one draw needn't show every extreme that they name: counts[c] cache slots of context index c are live, the first ones; some index has all 32 live in every draw. `offset`: at least the number of cache slots in all.
All inputs are finite; a program needn't handle non-finite values.
Results may differ from the reference program's by a relative error of at most 0.025.
Values may be sent and summed in bfloat16 or wider, within the bound.
No kernel may reach another device: no remote copies, remote signals or barrier semaphores. Data moves between devices by JAX's collectives and lax.ppermute only.
A program may use at most 128 MiB of HBM per device.

```python
import jax
import jax.numpy as jnp
from jax import lax

D = 7168
HEADS = 128
LATENT = 512
ROPE = 64
NOPE = 128
VDIM = 128
TOK_DEV = 128
CACHE_DEV = 32
TOKENS = 512
CACHE = 128
N_CTX = 4


def draw_group_latent(key, part):
    values = jnp.clip(jax.random.normal(jax.random.fold_in(key, 5), (TOKENS, LATENT + ROPE), jnp.float32), -4.0, 4.0)
    return values.astype(jnp.bfloat16)


def draw_q_rope(key, part):
    values = jnp.clip(jax.random.normal(jax.random.fold_in(key, 6), (TOKENS, HEADS * ROPE), jnp.float32), -4.0, 4.0)
    return values.astype(jnp.bfloat16)


def draw_counts(key, part):
    values = jax.random.randint(jax.random.fold_in(key, 7), (N_CTX,), 1, CACHE_DEV + 1)
    full_index = jax.random.randint(jax.random.fold_in(key, 8), (), 0, N_CTX)
    return jnp.where(jnp.arange(N_CTX) == full_index, CACHE_DEV, values).astype(jnp.int32)


def with_spikes(values, key, source, target, parts, factor):
    owner, partner = [(jnp.arange(values.shape[position]) // (values.shape[position] // parts)).reshape([-1 if axis == position else 1 for axis in range(values.ndim)]) for position in (source, target)]
    chosen = jax.random.permutation(key, parts)[partner]
    strong = (owner == chosen) | (owner == (partner + parts // 2) % parts)
    return jnp.where(strong, factor * values, values)


def block_scale(rng, extent, split, smallest, high):
    loudness, own = 1.0, jax.random.fold_in(rng, 6)
    for position, shards_of in split:
        heights = jnp.exp(jax.random.uniform(jax.random.fold_in(own, position), (shards_of,), jnp.float32, smallest / len(split), high / len(split)))
        loudness = loudness * jnp.repeat(heights, extent[position] // shards_of).reshape([-1 if axis == position else 1 for axis in range(len(extent))])
    return loudness


def scatter_about(stream_key, extent, spread, limit, shards=(), kind=jnp.bfloat16):
    result = jax.random.normal(stream_key, extent, jnp.float32) * spread
    if len(shards) > 0:
        result = block_scale(stream_key, extent, shards, -0.22, 0.18) * result
    return jnp.clip(result, min=-limit, max=limit).astype(kind)


def bell_draw_with(rng, dims, spread, limit, shards, heavy, kind=jnp.bfloat16):
    values = spread * jax.random.normal(rng, dims, jnp.float32)
    if shards:
        values = values * block_scale(rng, dims, shards, -0.22, 0.18)
    return jnp.clip(with_spikes(values, jax.random.fold_in(rng, 3), *heavy), -limit, limit).astype(kind)


def setup_inputs(seed: int = 0) -> dict:
    splits = jax.random.split(jax.random.key(seed), 10)
    q_nope = scatter_about(splits[0], (TOKENS, HEADS * NOPE), 1.0, 5.0, ((0, 4), (1, 8)))
    q_rope = draw_q_rope(jax.random.fold_in(splits[9], 71), 0)
    cache_latent = scatter_about(splits[2], (CACHE, LATENT + ROPE), 1.0, 4.0, ((0, 4),))
    group_latent = draw_group_latent(jax.random.fold_in(splits[9], 71), 0)
    offset = jax.random.randint(splits[4], (1,), N_CTX * CACHE_DEV, 2 * N_CTX * CACHE_DEV).astype(jnp.int32)
    counts = draw_counts(jax.random.fold_in(splits[9], 71), 0)
    up_key = scatter_about(splits[6], (HEADS, NOPE, LATENT), NOPE ** -0.5, 0.5, ((0, 8),))
    up_value = scatter_about(splits[7], (HEADS, LATENT, VDIM), LATENT ** -0.5, 0.25, ((0, 8),))
    out_weight = bell_draw_with(splits[8], (HEADS * VDIM, D), (HEADS * VDIM) ** -0.5, 0.0625, ((0, 8),), (0, 1, 8, 2.0))
    return dict(q_nope=q_nope, q_rope=q_rope, cache_latent=cache_latent, group_latent=group_latent, offset=offset, counts=counts, up_key=up_key, up_value=up_value, out_weight=out_weight)


def rotate(values, positions):
    half_width = values.shape[-1] // 2
    frequency = 10000.0 ** (-2.0 * jnp.arange(half_width, dtype=jnp.float32) / ROPE)
    angles = positions.astype(jnp.float32)[:, None] * frequency[None, :]
    cosine = jnp.cos(angles)
    sine_part = jnp.sin(angles)
    if values.ndim == 3:
        cosine = cosine[:, None, :]
        sine_part = sine_part[:, None, :]
    front_half = values[..., :half_width].astype(jnp.float32)
    back_half = values[..., half_width:].astype(jnp.float32)
    joined = jnp.concatenate([front_half * cosine - back_half * sine_part, back_half * cosine + front_half * sine_part], -1)
    return joined.astype(jnp.bfloat16)


def reference(q_nope, q_rope, cache_latent, group_latent, offset, counts, up_key, up_value, out_weight):
    positions = offset[0] + jnp.arange(TOKENS, dtype=jnp.int32)
    query_rope = rotate(q_rope.reshape(TOKENS, HEADS, ROPE), positions)
    key_rope = rotate(group_latent[:, LATENT:], positions)
    group_keys = jnp.concatenate([group_latent[:, :LATENT], key_rope], 1)
    span_rows = CACHE_DEV + TOK_DEV
    all_keys = jnp.concatenate([cache_latent.reshape(N_CTX, CACHE_DEV, LATENT + ROPE), group_keys.reshape(N_CTX, TOK_DEV, LATENT + ROPE)], 1)
    all_keys = all_keys.reshape(N_CTX * span_rows, LATENT + ROPE)
    key_index = jnp.arange(N_CTX * span_rows, dtype=jnp.int32)
    key_owner = key_index // span_rows
    key_slot = key_index % span_rows
    is_live = (key_slot < CACHE_DEV) & (key_slot < counts[key_owner])
    group_index = key_owner * TOK_DEV + key_slot - CACHE_DEV
    token_index = jnp.arange(TOKENS, dtype=jnp.int32)
    visible = is_live[None, :] | ((key_slot >= CACHE_DEV)[None, :] & (group_index[None, :] <= token_index[:, None]))
    score_scale = 1.0 / (NOPE + ROPE) ** 0.5
    latent_t = all_keys[:, :LATENT].T
    rope_t = all_keys[:, LATENT:].T
    latent_rows = all_keys[:, :LATENT]
    nope_heads = q_nope.reshape(TOKENS, HEADS, NOPE).transpose(1, 0, 2)
    rope_heads = query_rope.transpose(1, 0, 2)

    def one_head(inputs):
        nope_part, rope_part, key_weight, value_weight = inputs
        query_latent = jnp.dot(nope_part, key_weight, preferred_element_type=jnp.float32).astype(jnp.bfloat16)
        scores = jnp.dot(query_latent, latent_t, preferred_element_type=jnp.float32)
        scores = (scores + jnp.dot(rope_part, rope_t, preferred_element_type=jnp.float32)) * score_scale
        scores = jnp.where(visible, scores, -jnp.inf)
        row_max = jnp.max(scores, axis=1, keepdims=True)
        expos = jnp.exp(scores - row_max)
        row_sum = jnp.sum(expos, axis=1, keepdims=True)
        mixed = jnp.dot(expos.astype(jnp.bfloat16), latent_rows, preferred_element_type=jnp.float32) / row_sum
        attended = mixed.astype(jnp.bfloat16)
        return jnp.dot(attended, value_weight, preferred_element_type=jnp.float32).astype(jnp.bfloat16)

    head_out = lax.map(one_head, (nope_heads, rope_heads, up_key, up_value))
    joined = head_out.transpose(1, 0, 2).reshape(TOKENS, HEADS * VDIM)
    return jnp.dot(joined, out_weight, preferred_element_type=jnp.float32).astype(jnp.bfloat16)
```

```python
import functools
import math

import jax
import jax.numpy as jnp
from jax import lax
from jax.experimental import pallas as pl
from jax.experimental.pallas import tpu as pltpu
from jax.sharding import PartitionSpec as P

LATENT = 512
ROPE = 64
NOPE = 128
VDIM = 128
LANES = 128
HIDDEN = -1e30
LOG2E = 1.4426950408889634


def widen(width):
    return -(-width // LANES) * LANES


def rope_tables(positions, live):
    half = ROPE // 2
    frequency = 10000.0 ** (-2.0 * jnp.arange(half, dtype=jnp.float32) / ROPE)
    angles = positions.astype(jnp.float32)[:, None] * frequency[None, :]
    cosine = jnp.where(live[:, None], jnp.cos(angles), 1.0)
    sine = jnp.where(live[:, None], jnp.sin(angles), 0.0)
    return jnp.concatenate([cosine, cosine], 1), jnp.concatenate([-sine, sine], 1)


def query_kernel(nope_ref, rope_ref, up_ref, cos_ref, sin_ref, out_ref):
    heads = up_ref.shape[0]
    pad = out_ref.shape[2] - LATENT - ROPE
    half = ROPE // 2
    for head in range(heads):
        nope = nope_ref[:, head * NOPE : (head + 1) * NOPE]
        latent = jnp.dot(nope, up_ref[head], preferred_element_type=jnp.float32)
        out_ref[head, :, :LATENT] = latent.astype(jnp.bfloat16)
        raw = rope_ref[:, head * ROPE : (head + 1) * ROPE].astype(jnp.float32)
        swapped = jnp.concatenate([raw[:, half:], raw[:, :half]], 1)
        turned = raw * cos_ref[...] + swapped * sin_ref[...]
        filled = jnp.concatenate([turned, jnp.zeros((raw.shape[0], pad), jnp.float32)], 1)
        out_ref[head, :, LATENT:] = filled.astype(jnp.bfloat16)


def make_queries(q_nope, q_rope, up_key, cosine, sine):
    tokens = q_nope.shape[0]
    heads = up_key.shape[0]
    pair = LANES // ROPE
    width = widen(LATENT + ROPE)
    return pl.pallas_call(
        query_kernel,
        grid=(heads // pair,),
        in_specs=[
            pl.BlockSpec((tokens, pair * NOPE), lambda g: (0, g)),
            pl.BlockSpec((tokens, pair * ROPE), lambda g: (0, g)),
            pl.BlockSpec((pair, NOPE, LATENT), lambda g: (g, 0, 0)),
            pl.BlockSpec((tokens, ROPE), lambda g: (0, 0)),
            pl.BlockSpec((tokens, ROPE), lambda g: (0, 0)),
        ],
        out_specs=pl.BlockSpec((pair, tokens, width), lambda g: (g, 0, 0)),
        out_shape=jax.ShapeDtypeStruct((heads, tokens, width), jnp.bfloat16),
        name="queries",
        cost_estimate=pl.CostEstimate(
            flops=2 * heads * tokens * NOPE * LATENT, bytes_accessed=6 << 20, transcendentals=0
        ),
    )(q_nope, q_rope, up_key, cosine, sine)


def attend_kernel(
    q_ref, mine_ref, theirs_ref, cache_ref, group_ref, from_ref, cos_ref, sin_ref, row_ref, up_ref,
    out_ref, keys_ref,
):
    half = ROPE // 2
    shifts = mine_ref.shape[0]
    part_rows = mine_ref.shape[1]

    @pl.when(pl.program_id(0) == 0)
    def _():
        def put(raw, start):
            rows = raw.shape[0]
            keys_ref[start : start + rows, :LATENT] = raw[:, :LATENT]
            tail = raw[:, LATENT:].astype(jnp.float32)
            swapped = jnp.concatenate([tail[:, half:], tail[:, :half]], 1)
            turned = tail * cos_ref[start : start + rows] + swapped * sin_ref[start : start + rows]
            pad = keys_ref.shape[1] - LATENT - ROPE
            filled = jnp.concatenate([turned, jnp.zeros((rows, pad), jnp.float32)], 1)
            keys_ref[start : start + rows, LATENT:] = filled.astype(jnp.bfloat16)

        for shift in range(shifts):
            put(mine_ref[shift], 2 * shift * part_rows)
            put(theirs_ref[shift], (2 * shift + 1) * part_rows)
        base = 2 * shifts * part_rows
        put(cache_ref[...], base)
        put(group_ref[...], base + cache_ref.shape[0])

    heads, tokens, width = q_ref.shape
    queries = q_ref[...].reshape(heads * tokens, width)
    scores = lax.dot_general(
        queries, keys_ref[...], (((1,), (1,)), ((), ())), preferred_element_type=jnp.float32
    )
    scale = LOG2E / math.sqrt(NOPE + ROPE)
    visible = from_ref[...] <= row_ref[...]
    bias = jnp.where(visible, 0.0, HIDDEN)
    scores = scores.reshape(heads, tokens, -1) + bias[None]
    peak = jnp.max(scores, axis=2, keepdims=True)
    expos = jnp.exp2((scores - peak) * scale)
    total = jnp.sum(expos, axis=2, keepdims=True)
    weights = expos.astype(jnp.bfloat16).reshape(heads * tokens, -1)
    mixed = jnp.dot(weights, keys_ref[:, :LATENT], preferred_element_type=jnp.float32)
    attended = (mixed.reshape(heads, tokens, LATENT) / total).astype(jnp.bfloat16)
    for head in range(heads):
        value = jnp.dot(attended[head], up_ref[head], preferred_element_type=jnp.float32)
        out_ref[:, head * VDIM : (head + 1) * VDIM] = value.astype(jnp.bfloat16)


def attend(queries, mine, theirs, cache, group, visible_from, cosine, sine, rows, up_value):
    heads, tokens, width = queries.shape
    total = visible_from.shape[1]
    step = heads
    while step > 1 and step * tokens * total * 4 > (3 << 20) // 2:
        step //= 2
    whole = lambda a: pl.BlockSpec(a.shape, lambda g: (0,) * a.ndim)
    return pl.pallas_call(
        attend_kernel,
        grid=(heads // step,),
        in_specs=[
            pl.BlockSpec((step, tokens, width), lambda g: (g, 0, 0)),
            whole(mine),
            whole(theirs),
            whole(cache),
            whole(group),
            whole(visible_from),
            whole(cosine),
            whole(sine),
            whole(rows),
            pl.BlockSpec((step, LATENT, VDIM), lambda g: (g, 0, 0)),
        ],
        out_specs=pl.BlockSpec((tokens, step * VDIM), lambda g: (0, g)),
        out_shape=jax.ShapeDtypeStruct((tokens, heads * VDIM), jnp.bfloat16),
        scratch_shapes=[pltpu.VMEM((total, width), jnp.bfloat16)],
        name="attend",
        cost_estimate=pl.CostEstimate(
            flops=2 * heads * tokens * total * (LATENT + width),
            bytes_accessed=8 << 20,
            transcendentals=heads * tokens * total,
        ),
    )(queries, mine, theirs, cache, group, visible_from, cosine, sine, rows, up_value)


def project_kernel(order_ref, head_ref, weight_ref, out_ref):
    out_ref[0] = jnp.dot(
        head_ref[...], weight_ref[...], preferred_element_type=jnp.float32
    ).astype(jnp.bfloat16)


def project(order, head_out, weight, width):
    tokens, depth = head_out.shape
    blocks = order.shape[0]
    return pl.pallas_call(
        project_kernel,
        grid_spec=pltpu.PrefetchScalarGridSpec(
            num_scalar_prefetch=1,
            grid=(blocks,),
            in_specs=[
                pl.BlockSpec((tokens, depth), lambda i, order: (0, 0)),
                pl.BlockSpec((depth, width), lambda i, order: (0, order[i])),
            ],
            out_specs=pl.BlockSpec((1, tokens, width), lambda i, order: (i, 0, 0)),
        ),
        out_shape=jax.ShapeDtypeStruct((blocks, tokens, width), jnp.bfloat16),
        name="project",
        cost_estimate=pl.CostEstimate(
            flops=2 * blocks * tokens * depth * width,
            bytes_accessed=2 * blocks * depth * width,
            transcendentals=0,
        ),
    )(order, head_out, weight)


def local(ctx_size, tp_size, q_nope, q_rope, cache_latent, group_latent, offset, counts, up_key, up_value, out_weight):
    tokens = q_nope.shape[0]
    cached = cache_latent.shape[0]
    ctx = lax.axis_index("ctx")
    tp = lax.axis_index("tp")
    core = tp % 2
    swap = [(i, i ^ 1) for i in range(tp_size)]

    part = jnp.concatenate(
        [
            lax.dynamic_slice_in_dim(cache_latent, core * (cached // 2), cached // 2, 0),
            lax.dynamic_slice_in_dim(group_latent, core * (tokens // 2), tokens // 2, 0),
        ],
        0,
    )
    arrived = [
        lax.ppermute(part, "ctx", [(i, (i + shift) % ctx_size) for i in range(ctx_size)])
        for shift in range(1, ctx_size)
    ]
    mine = jnp.stack(arrived)
    theirs = lax.ppermute(mine, "tp", swap)

    part_rows = part.shape[0]
    slot = jnp.arange(part_rows, dtype=jnp.int32)
    owner = (ctx - jnp.arange(1, ctx_size, dtype=jnp.int32) + ctx_size) % ctx_size
    side = jnp.stack([core, 1 - core]).astype(jnp.int32)
    in_cache = slot < cached // 2
    cache_slot = side[:, None] * (cached // 2) + slot[None]
    group_slot = side[:, None] * (tokens // 2) + slot[None] - cached // 2
    far = jnp.int32(1 << 30)

    def marks(owners, cache_slots, group_slots, cache_mask):
        live = jnp.where(cache_slots < counts[owners], -1, far)
        position = owners * tokens + group_slots
        return jnp.where(cache_mask, live, position), position, ~cache_mask

    shape = (ctx_size - 1, 2, part_rows)
    remote = marks(
        jnp.broadcast_to(owner[:, None, None], shape),
        jnp.broadcast_to(cache_slot[None], shape),
        jnp.broadcast_to(group_slot[None], shape),
        jnp.broadcast_to(in_cache[None, None], shape),
    )
    own_slot = jnp.arange(cached + tokens, dtype=jnp.int32)
    own = marks(jnp.full_like(own_slot, ctx), own_slot, own_slot - cached, own_slot < cached)
    visible_from, position, rotated = (
        jnp.concatenate([a.reshape(-1), b]) for a, b in zip(remote, own)
    )
    key_cos, key_sin = rope_tables(offset[0] + position, rotated)
    rows = ctx * tokens + jnp.arange(tokens, dtype=jnp.int32)
    row_cos, row_sin = rope_tables(offset[0] + rows, jnp.ones((tokens,), bool))

    queries = make_queries(q_nope, q_rope, up_key, row_cos, row_sin)
    head_out = attend(
        queries, mine, theirs, cache_latent, group_latent, visible_from[None], key_cos, key_sin,
        rows[:, None], up_value,
    )

    features = out_weight.shape[1]
    width = features // tp_size
    chips = tp_size // 2
    if width % LANES or chips & (chips - 1):
        partial = jnp.dot(head_out, out_weight, preferred_element_type=jnp.float32)
        summed = lax.psum_scatter(
            partial.astype(jnp.bfloat16), "tp", scatter_dimension=1, tiled=True
        )
        return summed.astype(jnp.bfloat16)

    chip = tp // 2
    order = [delta for delta in range(chips - 1, -1, -1)]
    blocks = jnp.stack([2 * (chip ^ delta) for delta in order]).astype(jnp.int32)
    sent = project(blocks + (1 - core), head_out, out_weight, width)
    swapped = lax.ppermute(sent, "tp", swap)
    kept = project(blocks + core, head_out, out_weight, width)
    both = kept.astype(jnp.float32) + swapped.astype(jnp.float32)
    total = both[chips - 1]
    for place, delta in enumerate(order[:-1]):
        moved = lax.ppermute(
            both[place].astype(jnp.bfloat16), "tp", [(i, i ^ (2 * delta)) for i in range(tp_size)]
        )
        total = total + moved.astype(jnp.float32)
    return total.astype(jnp.bfloat16)


def solution(mesh):
    return jax.shard_map(
        functools.partial(local, mesh.shape["ctx"], mesh.shape["tp"]),
        mesh=mesh,
        in_specs=(
            P("ctx", "tp"),
            P("ctx", "tp"),
            P("ctx", None),
            P("ctx", None),
            P(),
            P(),
            P("tp", None, None),
            P("tp", None, None),
            P("tp", None),
        ),
        out_specs=P("ctx", "tp"),
        check_vma=False,
    )
```

```python
import functools
import math

import jax
import jax.numpy as jnp
from jax import lax
from jax.experimental import pallas as pl
from jax.experimental.pallas import tpu as pltpu
from jax.sharding import PartitionSpec as P


LATENT = 512
ROPE = 64
NOPE = 128
VDIM = 128
HALF = ROPE // 2
ENTRIES = LATENT + ROPE
LANES = 128
WIDE = -(-ENTRIES // LANES) * LANES
HIDDEN = -1e30
LOG2E = 1.4426950408889634
STREAMS = 8
MIB = 1 << 20


def in_hbm(*arrays):
    return [pltpu.with_memory_space_constraint(array, pltpu.HBM) for array in arrays]


def pack_kernel(group_ref, cache_ref, out_ref):
    core = lax.axis_index("tp") % 2
    features = group_ref.shape[0] // 2
    slots = cache_ref.shape[0] // 2
    out_ref[:features] = group_ref[pl.ds(pl.multiple_of(core * features, 16), features)]
    rows = cache_ref[pl.ds(pl.multiple_of(core * slots, 16), slots)]
    for tile in range(WIDE // LANES):
        piece = rows[:, tile * LANES : (tile + 1) * LANES]
        if piece.shape[1] < LANES:
            pad = jnp.zeros((slots, LANES - piece.shape[1]), piece.dtype)
            piece = jnp.concatenate([piece, pad], 1)
        start = features + tile * slots
        out_ref[start : start + slots] = piece


def pack(group_t, cache):
    slots = cache.shape[0] // 2
    rows = group_t.shape[0] // 2 + slots * (WIDE // LANES)
    return pl.pallas_call(
        pack_kernel,
        out_shape=jax.ShapeDtypeStruct((rows, group_t.shape[1]), jnp.bfloat16),
        name="pack",
        compiler_params=pltpu.CompilerParams(vmem_limit_bytes=4 * MIB),
    )(*in_hbm(group_t, cache))


def stream(source, base, target, sems):
    rows = target.shape[0] // STREAMS
    return [
        pltpu.make_async_copy(
            source.at[pl.ds(base + k * rows, rows)], target.at[pl.ds(k * rows, rows)], sems.at[k]
        )
        for k in range(STREAMS)
    ]


def front_kernel(fetch, offset_ref, nope_hbm, rope_hbm, up_hbm, *refs):
    if fetch:
        weight_ref, out_ref, cos_ref, sin_ref, stage_ref, *refs = refs
        *refs, stream_sems = refs
    else:
        out_ref, cos_ref, sin_ref, *refs = refs
    nope_ref, rope_ref, up_ref, turn_ref, sems = refs
    heads, tokens, _ = out_ref.shape
    pair = LANES // ROPE
    loads = [
        pltpu.make_async_copy(source, target, sems.at[k])
        for k, (source, target) in enumerate(
            [(rope_hbm, rope_ref), (nope_hbm, nope_ref), (up_hbm, up_ref)]
        )
    ]
    for copy in loads:
        copy.start()
    if fetch:
        streams = stream(weight_ref, 0, stage_ref, stream_sems)
        for copy in streams:
            copy.start()
    shape = cos_ref.shape
    position = offset_ref[0] + lax.broadcasted_iota(jnp.int32, shape, 1)
    index = lax.broadcasted_iota(jnp.int32, shape, 0).astype(jnp.float32)
    frequency = jnp.exp(index * (-2.0 * math.log(10000.0) / ROPE))
    angle = position.astype(jnp.float32) * frequency
    cos_ref[...] = jnp.cos(angle)
    sin_ref[...] = jnp.sin(angle)
    mine = pl.ds(pl.multiple_of(lax.axis_index("ctx") * tokens, LANES), tokens)
    cosine = cos_ref[:, mine]
    sine = sin_ref[:, mine]
    turn_ref[...] = jnp.concatenate([cosine, cosine, -sine, sine], 0).T
    for copy in loads:
        copy.wait()

    @pl.loop(0, heads // pair)
    def _(group):
        nope_at = pl.multiple_of(group * pair * NOPE, LANES)
        rope_at = pl.multiple_of(group * pair * ROPE, LANES)
        ropes = rope_ref[:, pl.ds(rope_at, pair * ROPE)].astype(jnp.float32)
        nopes = nope_ref[:, pl.ds(nope_at, pair * NOPE)]
        for head in range(pair):
            nope = nopes[:, head * NOPE : (head + 1) * NOPE]
            latent = jnp.dot(
                nope, up_ref[group * pair + head], preferred_element_type=jnp.float32
            )
            out_ref[group * pair + head, :, :LATENT] = latent.astype(jnp.bfloat16)
            raw = ropes[:, head * ROPE : (head + 1) * ROPE]
            swapped = jnp.concatenate([raw[:, HALF:], raw[:, :HALF]], 1)
            turned = raw * turn_ref[:, :ROPE] + swapped * turn_ref[:, ROPE:]
            pad = jnp.zeros((tokens, WIDE - ENTRIES), jnp.float32)
            filled = jnp.concatenate([turned, pad], 1)
            out_ref[group * pair + head, :, LATENT:] = filled.astype(jnp.bfloat16)

    if fetch:
        for copy in streams:
            copy.wait()


def front(ctx_size, offset, q_nope, q_rope, up_key, weight):
    tokens = q_nope.shape[0]
    heads = up_key.shape[0]
    vmem = pl.BlockSpec(memory_space=pltpu.VMEM)
    hbm = pl.BlockSpec(memory_space=pltpu.HBM)
    table = pltpu.VMEM((HALF, ctx_size * tokens), jnp.float32)
    in_specs = [pl.BlockSpec(memory_space=pltpu.SMEM), hbm, hbm, hbm]
    out_shape = [pltpu.VMEM((heads, tokens, WIDE), jnp.bfloat16), table, table]
    scratch = [
        pltpu.VMEM(q_nope.shape, q_nope.dtype),
        pltpu.VMEM(q_rope.shape, q_rope.dtype),
        pltpu.VMEM(up_key.shape, up_key.dtype),
        pltpu.VMEM((tokens, 2 * ROPE), jnp.float32),
        pltpu.SemaphoreType.DMA((3,)),
    ]
    args = [offset, q_nope, q_rope, up_key]
    if weight is not None:
        in_specs.append(hbm)
        out_shape.append(pltpu.VMEM(weight[1], weight[0].dtype))
        scratch.append(pltpu.SemaphoreType.DMA((STREAMS,)))
        args.append(weight[0])
    return pl.pallas_call(
        functools.partial(front_kernel, weight is not None),
        in_specs=in_specs,
        out_specs=[vmem] * len(out_shape),
        out_shape=out_shape,
        scratch_shapes=scratch,
        name="front",
        compiler_params=pltpu.CompilerParams(vmem_limit_bytes=8 * MIB),
        cost_estimate=pl.CostEstimate(
            flops=2 * heads * tokens * NOPE * LATENT, bytes_accessed=36 * MIB, transcendentals=0
        ),
    )(args[0], *in_hbm(*args[1:]))


def attend_kernel(step, first, counts_ref, q_ref, mine_ref, theirs_ref, cache_ref, group_ref, *refs):
    if first is None:
        cos_ref, sin_ref, up_ref, out_ref, keys_ref, bias_ref, cached_ref = refs
    else:
        cos_ref, sin_ref, up_ref, weight_ref, out_ref, stage_ref, *refs = refs
        keys_ref, bias_ref, cached_ref, sems = refs
        streams = stream(weight_ref, first, stage_ref, sems)
        for copy in streams:
            copy.start()
    shifts = mine_ref.shape[0]
    size = shifts + 1
    slots, tokens = cache_ref.shape[0], group_ref.shape[1]
    features = ENTRIES // 2
    tiles = WIDE // LANES
    ctx = lax.axis_index("ctx")
    core = lax.axis_index("tp") % 2
    keys_ref[ENTRIES:] = jnp.zeros((WIDE - ENTRIES, keys_ref.shape[1]), jnp.bfloat16)
    cached_ref[:slots, :ENTRIES] = cache_ref[...].astype(jnp.float32)
    cached_ref[:, ENTRIES:] = jnp.zeros((size * slots, WIDE - ENTRIES), jnp.float32)
    keys_ref[:ENTRIES, :tokens] = group_ref[...]
    for shift in range(shifts):
        lanes = slice((shift + 1) * tokens, (shift + 2) * tokens)
        for side, part in ((core, mine_ref), (1 - core, theirs_ref)):
            start = pl.multiple_of(side * features, 16)
            keys_ref[pl.ds(start, features), lanes] = part[shift, :features]
            start = pl.multiple_of((shift + 1) * slots + side * (slots // 2), 16)
            for tile in range(tiles):
                base = features + tile * (slots // 2)
                piece = part[shift, base : base + slots // 2].astype(jnp.float32)
                cached_ref[pl.ds(start, slots // 2), tile * LANES : (tile + 1) * LANES] = piece
    row = lax.broadcasted_iota(jnp.int32, (tokens, tokens), 0)
    lane = lax.broadcasted_iota(jnp.int32, (tokens, tokens), 1)
    bias_ref[:, :tokens] = jnp.where(lane <= row, 0.0, HIDDEN)
    slot = lax.broadcasted_iota(jnp.int32, (tokens, size * slots), 1)
    limit = jnp.full(slot.shape, counts_ref[ctx], jnp.int32)
    for shift in range(size):
        owner = lax.rem(ctx - shift + size, size)
        lanes = slice(shift * tokens, (shift + 1) * tokens)
        if shift > 0:
            shown = jnp.where(owner < ctx, 0.0, HIDDEN)
            bias_ref[:, lanes] = jnp.full((tokens, tokens), shown, jnp.float32)
            limit = jnp.where(slot >= shift * slots, shift * slots + counts_ref[owner], limit)
        where = pl.ds(pl.multiple_of(owner * tokens, LANES), tokens)
        cosine = cos_ref[:, where]
        sine = sin_ref[:, where]
        ahead = keys_ref[LATENT : LATENT + HALF, lanes].astype(jnp.float32)
        behind = keys_ref[LATENT + HALF : ENTRIES, lanes].astype(jnp.float32)
        keys_ref[LATENT : LATENT + HALF, lanes] = (ahead * cosine - behind * sine).astype(
            jnp.bfloat16
        )
        keys_ref[LATENT + HALF : ENTRIES, lanes] = (behind * cosine + ahead * sine).astype(
            jnp.bfloat16
        )
    bias_ref[:, size * tokens :] = jnp.where(slot < limit, 0.0, HIDDEN)
    keys_ref[:, size * tokens :] = cached_ref[...].T.astype(jnp.bfloat16)

    width = q_ref.shape[2]
    scale = LOG2E / math.sqrt(NOPE + ROPE)

    @pl.loop(0, q_ref.shape[0] // step)
    def _(group):
        queries = q_ref[pl.ds(group * step, step)].reshape(step * tokens, width)
        scores = jnp.dot(queries, keys_ref[...], preferred_element_type=jnp.float32)
        scores = scores.reshape(step, tokens, -1) + bias_ref[...][None]
        peak = jnp.max(scores, axis=2, keepdims=True)
        expos = jnp.exp2((scores - peak) * scale)
        total = jnp.sum(expos, axis=2, keepdims=True)
        weights = expos.astype(jnp.bfloat16).reshape(step * tokens, -1)
        mixed = lax.dot_general(
            weights, keys_ref[:LATENT], (((1,), (1,)), ((), ())), preferred_element_type=jnp.float32
        )
        attended = (mixed.reshape(step, tokens, LATENT) / total).astype(jnp.bfloat16)
        values = [
            jnp.dot(attended[head], up_ref[group * step + head], preferred_element_type=jnp.float32)
            for head in range(step)
        ]
        lanes = pl.ds(pl.multiple_of(group * step * VDIM, LANES), step * VDIM)
        out_ref[:, lanes] = jnp.concatenate(values, 1).astype(jnp.bfloat16)

    if first is not None:
        for copy in streams:
            copy.wait()


def attend(counts, queries, mine, theirs, cache, group_t, cosine, sine, up_value, weight, base):
    heads, tokens, width = queries.shape
    size = mine.shape[0] + 1
    slots = cache.shape[0]
    total = size * (tokens + slots)
    step = heads
    while step > 1 and step * tokens * total * 4 > 3 * MIB // 2:
        step //= 2
    vmem = pl.BlockSpec(memory_space=pltpu.VMEM)
    in_specs = [pl.BlockSpec(memory_space=pltpu.SMEM)] + [vmem] * 8
    out_shape = [pltpu.VMEM((tokens, heads * VDIM), jnp.bfloat16)]
    scratch = [
        pltpu.VMEM((WIDE, total), jnp.bfloat16),
        pltpu.VMEM((tokens, total), jnp.float32),
        pltpu.VMEM((size * slots, WIDE), jnp.float32),
    ]
    args = [counts, queries, mine, theirs, cache, group_t, cosine, sine, up_value]
    if base is not None:
        in_specs.append(pl.BlockSpec(memory_space=pltpu.HBM))
        out_shape.append(pltpu.VMEM((weight.shape[0] - base, weight.shape[1]), weight.dtype))
        scratch.append(pltpu.SemaphoreType.DMA((STREAMS,)))
        args += in_hbm(weight)
    return pl.pallas_call(
        functools.partial(attend_kernel, step, base),
        in_specs=in_specs,
        out_specs=[vmem] * len(out_shape),
        out_shape=out_shape,
        scratch_shapes=scratch,
        name="attend",
        compiler_params=pltpu.CompilerParams(vmem_limit_bytes=10 * MIB + total * 8192),
        cost_estimate=pl.CostEstimate(
            flops=2 * heads * tokens * total * (LATENT + width),
            bytes_accessed=8 * MIB,
            transcendentals=heads * tokens * total,
        ),
    )(*args)


def project_kernel(width, deltas, theirs, add, head_ref, upper_ref, lower_ref, *refs):
    tp = lax.axis_index("tp")
    side = 1 - tp % 2 if theirs else tp % 2
    count = len(deltas)
    outs = refs[count if add else 0 :]
    for place, delta in enumerate(deltas):
        start = pl.multiple_of((((tp // 2) ^ delta) * 2 + side) * width, LANES)
        lanes = pl.ds(start, width)
        split = upper_ref.shape[0]
        block = jnp.dot(
            head_ref[:, :split], upper_ref[:, lanes], preferred_element_type=jnp.float32
        ) + jnp.dot(head_ref[:, split:], lower_ref[:, lanes], preferred_element_type=jnp.float32)
        if add:
            block = block + refs[place][...].astype(jnp.float32)
        outs[place][...] = block.astype(jnp.bfloat16)


def project(head_out, upper, lower, width, deltas, theirs, arrived=()):
    tokens, depth = head_out.shape
    out = jax.ShapeDtypeStruct((tokens, width), jnp.bfloat16)
    return pl.pallas_call(
        functools.partial(project_kernel, width, deltas, theirs, bool(arrived)),
        in_specs=[pl.BlockSpec(memory_space=pltpu.VMEM)] * (3 + len(arrived)),
        out_specs=[pl.BlockSpec(memory_space=pltpu.VMEM)] * len(deltas),
        out_shape=[out] * len(deltas),
        name="project",
        compiler_params=pltpu.CompilerParams(vmem_limit_bytes=6 * MIB),
        cost_estimate=pl.CostEstimate(
            flops=2 * len(deltas) * tokens * depth * width,
            bytes_accessed=2 * len(deltas) * tokens * width,
            transcendentals=0,
        ),
    )(head_out, upper, lower, *arrived)


def layer(
    ctx_size, tp_size, q_nope, q_rope, cache_latent, group_latent, offset, counts, up_key, up_value,
    out_weight,
):
    width = out_weight.shape[1] // tp_size
    chips = tp_size // 2
    direct = width % LANES == 0 and chips & (chips - 1) == 0
    swap = [(i, i ^ 1) for i in range(tp_size)]

    group_t = group_latent.T
    part = pack(group_t, cache_latent)
    arrived = []
    for shift in range(1, ctx_size):
        ring = [(i, (i + shift) % ctx_size) for i in range(ctx_size)]
        arrived.append(lax.ppermute(part, "ctx", ring))
    mine = jnp.stack(arrived)
    theirs = lax.ppermute(mine, "tp", swap)
    depth, columns = out_weight.shape
    base = depth // 2 if direct else None
    weight = (out_weight, (base, columns)) if direct else None
    queries, cosine, sine, *upper = front(ctx_size, offset, q_nope, q_rope, up_key, weight)
    head_out, *lower = attend(
        counts, queries, mine, theirs, cache_latent, group_t, cosine, sine, up_value, out_weight,
        base,
    )
    if not direct:
        partial = jnp.dot(head_out, out_weight, preferred_element_type=jnp.float32)
        summed = lax.psum_scatter(
            partial.astype(jnp.bfloat16), "tp", scatter_dimension=1, tiled=True
        )
        return summed.astype(jnp.bfloat16)

    groups = [[chips - 1], list(range(1, chips - 1)), [0]]
    arrived = []
    for deltas in groups:
        sent = project(head_out, upper[0], lower[0], width, deltas, True)
        arrived.append([lax.ppermute(block, "tp", swap) for block in sent])
    moved = []
    for deltas, blocks in zip(groups, arrived):
        sums = project(head_out, upper[0], lower[0], width, deltas, False, tuple(blocks))
        for delta, block in zip(deltas, sums):
            if delta:
                block = lax.ppermute(block, "tp", [(i, i ^ (2 * delta)) for i in range(tp_size)])
            moved.append(block.astype(jnp.float32))
    return sum(moved).astype(jnp.bfloat16)


def solution(mesh):
    return jax.shard_map(
        functools.partial(layer, mesh.shape["ctx"], mesh.shape["tp"]),
        mesh=mesh,
        in_specs=(
            P("ctx", "tp"),
            P("ctx", "tp"),
            P("ctx", None),
            P("ctx", None),
            P(),
            P(),
            P("tp", None, None),
            P("tp", None, None),
            P("tp", None),
        ),
        out_specs=P("ctx", "tp"),
        check_vma=False,
    )
```

```python
import functools
import math

import jax
import jax.numpy as jnp
from jax import lax
from jax.experimental import pallas as pl
from jax.experimental.pallas import tpu as pltpu
from jax.sharding import PartitionSpec as P


LATENT = 512
ROPE = 64
NOPE = 128
VDIM = 128
HALF = ROPE // 2
ENTRIES = LATENT + ROPE
LANES = 128
WIDE = -(-ENTRIES // LANES) * LANES
HIDDEN = -1e30
LOG2E = 1.4426950408889634
STREAMS = 8
MIB = 1 << 20


def in_hbm(*arrays):
    return [pltpu.with_memory_space_constraint(array, pltpu.HBM) for array in arrays]


def pack_kernel(group_ref, cache_ref, out_ref):
    core = lax.axis_index("tp") % 2
    features = group_ref.shape[0] // 2
    slots = cache_ref.shape[0] // 2
    out_ref[:features] = group_ref[pl.ds(pl.multiple_of(core * features, 16), features)]
    rows = cache_ref[pl.ds(pl.multiple_of(core * slots, 16), slots)]
    for tile in range(WIDE // LANES):
        piece = rows[:, tile * LANES : (tile + 1) * LANES]
        if piece.shape[1] < LANES:
            pad = jnp.zeros((slots, LANES - piece.shape[1]), piece.dtype)
            piece = jnp.concatenate([piece, pad], 1)
        start = features + tile * slots
        out_ref[start : start + slots] = piece


def pack(group_t, cache):
    slots = cache.shape[0] // 2
    rows = group_t.shape[0] // 2 + slots * (WIDE // LANES)
    return pl.pallas_call(
        pack_kernel,
        out_shape=jax.ShapeDtypeStruct((rows, group_t.shape[1]), jnp.bfloat16),
        name="pack",
        compiler_params=pltpu.CompilerParams(vmem_limit_bytes=4 * MIB),
    )(*in_hbm(group_t, cache))


def stream(source, base, target, sems):
    rows = target.shape[0] // STREAMS
    return [
        pltpu.make_async_copy(
            source.at[pl.ds(base + k * rows, rows)], target.at[pl.ds(k * rows, rows)], sems.at[k]
        )
        for k in range(STREAMS)
    ]


def front_kernel(fetch, offset_ref, nope_hbm, rope_hbm, up_hbm, *refs):
    if fetch:
        weight_ref, out_ref, cos_ref, sin_ref, stage_ref, *refs = refs
        *refs, stream_sems = refs
    else:
        out_ref, cos_ref, sin_ref, *refs = refs
    nope_ref, rope_ref, up_ref, turn_ref, sems = refs
    heads, tokens, _ = out_ref.shape
    pair = LANES // ROPE
    loads = [
        pltpu.make_async_copy(source, target, sems.at[k])
        for k, (source, target) in enumerate(
            [(rope_hbm, rope_ref), (nope_hbm, nope_ref), (up_hbm, up_ref)]
        )
    ]
    for copy in loads:
        copy.start()
    if fetch:
        streams = stream(weight_ref, 0, stage_ref, stream_sems)
        for copy in streams:
            copy.start()
    shape = cos_ref.shape
    position = offset_ref[0] + lax.broadcasted_iota(jnp.int32, shape, 1)
    index = lax.broadcasted_iota(jnp.int32, shape, 0).astype(jnp.float32)
    frequency = jnp.exp(index * (-2.0 * math.log(10000.0) / ROPE))
    angle = position.astype(jnp.float32) * frequency
    cos_ref[...] = jnp.cos(angle)
    sin_ref[...] = jnp.sin(angle)
    mine = pl.ds(pl.multiple_of(lax.axis_index("ctx") * tokens, LANES), tokens)
    cosine = cos_ref[:, mine]
    sine = sin_ref[:, mine]
    turn_ref[...] = jnp.concatenate([cosine, cosine, -sine, sine], 0).T
    for copy in loads:
        copy.wait()

    @pl.loop(0, heads // pair)
    def _(group):
        nope_at = pl.multiple_of(group * pair * NOPE, LANES)
        rope_at = pl.multiple_of(group * pair * ROPE, LANES)
        ropes = rope_ref[:, pl.ds(rope_at, pair * ROPE)].astype(jnp.float32)
        nopes = nope_ref[:, pl.ds(nope_at, pair * NOPE)]
        for head in range(pair):
            nope = nopes[:, head * NOPE : (head + 1) * NOPE]
            latent = jnp.dot(
                nope, up_ref[group * pair + head], preferred_element_type=jnp.float32
            )
            out_ref[group * pair + head, :, :LATENT] = latent.astype(jnp.bfloat16)
            raw = ropes[:, head * ROPE : (head + 1) * ROPE]
            swapped = jnp.concatenate([raw[:, HALF:], raw[:, :HALF]], 1)
            turned = raw * turn_ref[:, :ROPE] + swapped * turn_ref[:, ROPE:]
            pad = jnp.zeros((tokens, WIDE - ENTRIES), jnp.float32)
            filled = jnp.concatenate([turned, pad], 1)
            out_ref[group * pair + head, :, LATENT:] = filled.astype(jnp.bfloat16)

    if fetch:
        for copy in streams:
            copy.wait()


def front(ctx_size, offset, q_nope, q_rope, up_key, weight):
    tokens = q_nope.shape[0]
    heads = up_key.shape[0]
    vmem = pl.BlockSpec(memory_space=pltpu.VMEM)
    hbm = pl.BlockSpec(memory_space=pltpu.HBM)
    table = pltpu.VMEM((HALF, ctx_size * tokens), jnp.float32)
    in_specs = [pl.BlockSpec(memory_space=pltpu.SMEM), hbm, hbm, hbm]
    out_shape = [pltpu.VMEM((heads, tokens, WIDE), jnp.bfloat16), table, table]
    scratch = [
        pltpu.VMEM(q_nope.shape, q_nope.dtype),
        pltpu.VMEM(q_rope.shape, q_rope.dtype),
        pltpu.VMEM(up_key.shape, up_key.dtype),
        pltpu.VMEM((tokens, 2 * ROPE), jnp.float32),
        pltpu.SemaphoreType.DMA((3,)),
    ]
    args = [offset, q_nope, q_rope, up_key]
    if weight is not None:
        in_specs.append(hbm)
        out_shape.append(pltpu.VMEM(weight[1], weight[0].dtype))
        scratch.append(pltpu.SemaphoreType.DMA((STREAMS,)))
        args.append(weight[0])
    return pl.pallas_call(
        functools.partial(front_kernel, weight is not None),
        in_specs=in_specs,
        out_specs=[vmem] * len(out_shape),
        out_shape=out_shape,
        scratch_shapes=scratch,
        name="front",
        compiler_params=pltpu.CompilerParams(vmem_limit_bytes=8 * MIB),
        cost_estimate=pl.CostEstimate(
            flops=2 * heads * tokens * NOPE * LATENT, bytes_accessed=36 * MIB, transcendentals=0
        ),
    )(args[0], *in_hbm(*args[1:]))


def attend_kernel(step, first, counts_ref, q_ref, mine_ref, theirs_ref, cache_ref, group_ref, *refs):
    if first is None:
        cos_ref, sin_ref, up_ref, out_ref, keys_ref, bias_ref, cached_ref = refs
    else:
        cos_ref, sin_ref, up_ref, weight_ref, out_ref, stage_ref, *refs = refs
        keys_ref, bias_ref, cached_ref, sems = refs
        streams = stream(weight_ref, first, stage_ref, sems)
        for copy in streams:
            copy.start()
    shifts = mine_ref.shape[0]
    size = shifts + 1
    slots, tokens = cache_ref.shape[0], group_ref.shape[1]
    features = ENTRIES // 2
    tiles = WIDE // LANES
    ctx = lax.axis_index("ctx")
    core = lax.axis_index("tp") % 2
    keys_ref[ENTRIES:] = jnp.zeros((WIDE - ENTRIES, keys_ref.shape[1]), jnp.bfloat16)
    cached_ref[:slots, :ENTRIES] = cache_ref[...].astype(jnp.float32)
    cached_ref[:, ENTRIES:] = jnp.zeros((size * slots, WIDE - ENTRIES), jnp.float32)
    keys_ref[:ENTRIES, :tokens] = group_ref[...]
    for shift in range(shifts):
        lanes = slice((shift + 1) * tokens, (shift + 2) * tokens)
        for side, part in ((core, mine_ref), (1 - core, theirs_ref)):
            start = pl.multiple_of(side * features, 16)
            keys_ref[pl.ds(start, features), lanes] = part[shift, :features]
            start = pl.multiple_of((shift + 1) * slots + side * (slots // 2), 16)
            for tile in range(tiles):
                base = features + tile * (slots // 2)
                piece = part[shift, base : base + slots // 2].astype(jnp.float32)
                cached_ref[pl.ds(start, slots // 2), tile * LANES : (tile + 1) * LANES] = piece
    row = lax.broadcasted_iota(jnp.int32, (tokens, tokens), 0)
    lane = lax.broadcasted_iota(jnp.int32, (tokens, tokens), 1)
    bias_ref[:, :tokens] = jnp.where(lane <= row, 0.0, HIDDEN)
    slot = lax.broadcasted_iota(jnp.int32, (tokens, size * slots), 1)
    limit = jnp.full(slot.shape, counts_ref[ctx], jnp.int32)
    for shift in range(size):
        owner = lax.rem(ctx - shift + size, size)
        lanes = slice(shift * tokens, (shift + 1) * tokens)
        if shift > 0:
            shown = jnp.where(owner < ctx, 0.0, HIDDEN)
            bias_ref[:, lanes] = jnp.full((tokens, tokens), shown, jnp.float32)
            limit = jnp.where(slot >= shift * slots, shift * slots + counts_ref[owner], limit)
        where = pl.ds(pl.multiple_of(owner * tokens, LANES), tokens)
        cosine = cos_ref[:, where]
        sine = sin_ref[:, where]
        ahead = keys_ref[LATENT : LATENT + HALF, lanes].astype(jnp.float32)
        behind = keys_ref[LATENT + HALF : ENTRIES, lanes].astype(jnp.float32)
        keys_ref[LATENT : LATENT + HALF, lanes] = (ahead * cosine - behind * sine).astype(
            jnp.bfloat16
        )
        keys_ref[LATENT + HALF : ENTRIES, lanes] = (behind * cosine + ahead * sine).astype(
            jnp.bfloat16
        )
    bias_ref[:, size * tokens :] = jnp.where(slot < limit, 0.0, HIDDEN)
    keys_ref[:, size * tokens :] = cached_ref[...].T.astype(jnp.bfloat16)

    width = q_ref.shape[2]
    scale = LOG2E / math.sqrt(NOPE + ROPE)

    @pl.loop(0, q_ref.shape[0] // step)
    def _(group):
        queries = q_ref[pl.ds(group * step, step)].reshape(step * tokens, width)
        scores = jnp.dot(queries, keys_ref[...], preferred_element_type=jnp.float32)
        scores = scores.reshape(step, tokens, -1) + bias_ref[...][None]
        peak = jnp.max(scores, axis=2, keepdims=True)
        expos = jnp.exp2((scores - peak) * scale)
        total = jnp.sum(expos, axis=2, keepdims=True)
        weights = expos.astype(jnp.bfloat16).reshape(step * tokens, -1)
        mixed = lax.dot_general(
            weights, keys_ref[:LATENT], (((1,), (1,)), ((), ())), preferred_element_type=jnp.float32
        )
        attended = (mixed.reshape(step, tokens, LATENT) / total).astype(jnp.bfloat16)
        values = [
            jnp.dot(attended[head], up_ref[group * step + head], preferred_element_type=jnp.float32)
            for head in range(step)
        ]
        lanes = pl.ds(pl.multiple_of(group * step * VDIM, LANES), step * VDIM)
        out_ref[:, lanes] = jnp.concatenate(values, 1).astype(jnp.bfloat16)

    if first is not None:
        for copy in streams:
            copy.wait()


def attend(counts, queries, mine, theirs, cache, group_t, cosine, sine, up_value, weight, base):
    heads, tokens, width = queries.shape
    size = mine.shape[0] + 1
    slots = cache.shape[0]
    total = size * (tokens + slots)
    step = heads
    while step > 1 and step * tokens * total * 4 > 3 * MIB:
        step //= 2
    vmem = pl.BlockSpec(memory_space=pltpu.VMEM)
    in_specs = [pl.BlockSpec(memory_space=pltpu.SMEM)] + [vmem] * 8
    out_shape = [pltpu.VMEM((tokens, heads * VDIM), jnp.bfloat16)]
    scratch = [
        pltpu.VMEM((WIDE, total), jnp.bfloat16),
        pltpu.VMEM((tokens, total), jnp.float32),
        pltpu.VMEM((size * slots, WIDE), jnp.float32),
    ]
    args = [counts, queries, mine, theirs, cache, group_t, cosine, sine, up_value]
    if base is not None:
        in_specs.append(pl.BlockSpec(memory_space=pltpu.HBM))
        out_shape.append(pltpu.VMEM((weight.shape[0] - base, weight.shape[1]), weight.dtype))
        scratch.append(pltpu.SemaphoreType.DMA((STREAMS,)))
        args += in_hbm(weight)
    return pl.pallas_call(
        functools.partial(attend_kernel, step, base),
        in_specs=in_specs,
        out_specs=[vmem] * len(out_shape),
        out_shape=out_shape,
        scratch_shapes=scratch,
        name="attend",
        compiler_params=pltpu.CompilerParams(vmem_limit_bytes=10 * MIB + total * 8192),
        cost_estimate=pl.CostEstimate(
            flops=2 * heads * tokens * total * (LATENT + width),
            bytes_accessed=8 * MIB,
            transcendentals=heads * tokens * total,
        ),
    )(*args)


def project_kernel(width, deltas, theirs, add, parts, head_ref, upper_ref, lower_ref, *refs):
    tp = lax.axis_index("tp")
    side = 1 - tp % 2 if theirs else tp % 2
    split = upper_ref.shape[0]
    outs = refs[len(deltas) if add else 0 :]
    for place, delta in enumerate(deltas):
        start = pl.multiple_of((((tp // 2) ^ delta) * 2 + side) * width, LANES)
        lanes = pl.ds(start, width)
        block = jnp.dot(
            head_ref[:, :split], upper_ref[:, lanes], preferred_element_type=jnp.float32
        ) + jnp.dot(head_ref[:, split:], lower_ref[:, lanes], preferred_element_type=jnp.float32)
        if add:
            block = block + refs[place][...].astype(jnp.float32)
        block = block.astype(jnp.bfloat16)
        rows = block.shape[0] // parts
        for part in range(parts):
            outs[place * parts + part][...] = block[part * rows : (part + 1) * rows]


def project(head_out, upper, lower, width, deltas, theirs, arrived=(), parts=1):
    tokens, depth = head_out.shape
    out = jax.ShapeDtypeStruct((tokens // parts, width), jnp.bfloat16)
    count = len(deltas) * parts
    return pl.pallas_call(
        functools.partial(project_kernel, width, deltas, theirs, bool(arrived), parts),
        in_specs=[pl.BlockSpec(memory_space=pltpu.VMEM)] * (3 + len(arrived)),
        out_specs=[pl.BlockSpec(memory_space=pltpu.VMEM)] * count,
        out_shape=[out] * count,
        name="project",
        compiler_params=pltpu.CompilerParams(vmem_limit_bytes=6 * MIB),
        cost_estimate=pl.CostEstimate(
            flops=2 * len(deltas) * tokens * depth * width,
            bytes_accessed=2 * len(deltas) * tokens * width,
            transcendentals=0,
        ),
    )(head_out, upper, lower, *arrived)


def layer(
    ctx_size, tp_size, q_nope, q_rope, cache_latent, group_latent, offset, counts, up_key, up_value,
    out_weight,
):
    width = out_weight.shape[1] // tp_size
    chips = tp_size // 2
    direct = width % LANES == 0 and chips == 4
    swap = [(i, i ^ 1) for i in range(tp_size)]

    group_t = group_latent.T
    part = pack(group_t, cache_latent)
    arrived = []
    for shift in range(1, ctx_size):
        ring = [(i, (i + shift) % ctx_size) for i in range(ctx_size)]
        arrived.append(lax.ppermute(part, "ctx", ring))
    mine = jnp.stack(arrived)
    theirs = lax.ppermute(mine, "tp", swap)
    depth, columns = out_weight.shape
    base = depth // 2 if direct else None
    weight = (out_weight, (base, columns)) if direct else None
    queries, cosine, sine, *upper = front(ctx_size, offset, q_nope, q_rope, up_key, weight)
    head_out, *lower = attend(
        counts, queries, mine, theirs, cache_latent, group_t, cosine, sine, up_value, out_weight,
        base,
    )
    if not direct:
        partial = jnp.dot(head_out, out_weight, preferred_element_type=jnp.float32)
        summed = lax.psum_scatter(
            partial.astype(jnp.bfloat16), "tp", scatter_dimension=1, tiled=True
        )
        return summed.astype(jnp.bfloat16)

    def move(block, delta):
        return lax.ppermute(block, "tp", [(i, i ^ delta) for i in range(tp_size)])

    def plus(first, second):
        return (first.astype(jnp.float32) + second.astype(jnp.float32)).astype(jnp.bfloat16)

    run = functools.partial(project, upper=upper[0], lower=lower[0], width=width)
    far = [move(block, 1) for block in run(head_out, deltas=[3], theirs=True)]
    near = [move(block, 1) for block in run(head_out, deltas=[1, 2], theirs=True)]
    far_top, far_low = run(head_out, deltas=[3], theirs=False, arrived=far, parts=2)
    via_first = move(far_top, 2)
    via_second = move(far_low, 4)
    first_top, first_low, second_top, second_low = run(
        head_out, deltas=[1, 2], theirs=False, arrived=near, parts=2
    )
    got_first_top = move(first_top, 2)
    got_second_low = move(second_low, 4)
    later, first_low, second_top = lax.optimization_barrier((head_out, first_low, second_top))
    own = [move(block, 1) for block in run(later, deltas=[0], theirs=True)]
    got_first_low = move(plus(first_low, via_second), 2)
    got_second_top = move(plus(second_top, via_first), 4)
    own_top, own_low = run(later, deltas=[0], theirs=False, arrived=own, parts=2)
    halves = [(own_top, got_first_top, got_second_top), (own_low, got_first_low, got_second_low)]
    summed = [sum(block.astype(jnp.float32) for block in half) for half in halves]
    return jnp.concatenate(summed, 0).astype(jnp.bfloat16)


def solution(mesh):
    return jax.shard_map(
        functools.partial(layer, mesh.shape["ctx"], mesh.shape["tp"]),
        mesh=mesh,
        in_specs=(
            P("ctx", "tp"),
            P("ctx", "tp"),
            P("ctx", None),
            P("ctx", None),
            P(),
            P(),
            P("tp", None, None),
            P("tp", None, None),
            P("tp", None),
        ),
        out_specs=P("ctx", "tp"),
        check_vma=False,
    )
```

```python
import functools
import math

import jax
import jax.numpy as jnp
from jax import lax
from jax.experimental import pallas as pl
from jax.experimental.pallas import tpu as pltpu
from jax.sharding import PartitionSpec as P


LATENT = 512
ROPE = 64
NOPE = 128
VDIM = 128
HALF = ROPE // 2
ENTRIES = LATENT + ROPE
LANES = 128
WIDE = -(-ENTRIES // LANES) * LANES
HIDDEN = -1e30
LOG2E = 1.4426950408889634
STREAMS = 8
SCALE = LOG2E / math.sqrt(NOPE + ROPE)
MIB = 1 << 20


def in_hbm(*arrays):
    return [pltpu.with_memory_space_constraint(array, pltpu.HBM) for array in arrays]


def pack_kernel(group_ref, cache_ref, out_ref):
    core = lax.axis_index("tp") % 2
    features = group_ref.shape[0] // 2
    slots = cache_ref.shape[0] // 2
    out_ref[:features] = group_ref[pl.ds(pl.multiple_of(core * features, 16), features)]
    rows = cache_ref[pl.ds(pl.multiple_of(core * slots, 16), slots)]
    for tile in range(WIDE // LANES):
        piece = rows[:, tile * LANES : (tile + 1) * LANES]
        if piece.shape[1] < LANES:
            pad = jnp.zeros((slots, LANES - piece.shape[1]), piece.dtype)
            piece = jnp.concatenate([piece, pad], 1)
        start = features + tile * slots
        out_ref[start : start + slots] = piece


def pack(group_t, cache):
    slots = cache.shape[0] // 2
    rows = group_t.shape[0] // 2 + slots * (WIDE // LANES)
    return pl.pallas_call(
        pack_kernel,
        out_shape=jax.ShapeDtypeStruct((rows, group_t.shape[1]), jnp.bfloat16),
        name="pack",
        compiler_params=pltpu.CompilerParams(vmem_limit_bytes=4 * MIB),
    )(*in_hbm(group_t, cache))


def stream(source, base, target, sems):
    rows = target.shape[0] // STREAMS
    return [
        pltpu.make_async_copy(
            source.at[pl.ds(base + k * rows, rows)], target.at[pl.ds(k * rows, rows)], sems.at[k]
        )
        for k in range(STREAMS)
    ]


def front_kernel(fetch, offset_ref, nope_hbm, rope_hbm, up_hbm, *refs):
    if fetch:
        weight_ref, out_ref, cos_ref, sin_ref, stage_ref, *refs = refs
        *refs, stream_sems = refs
    else:
        out_ref, cos_ref, sin_ref, *refs = refs
    nope_ref, rope_ref, up_ref, turn_ref, sems = refs
    heads, tokens, _ = out_ref.shape
    pair = LANES // ROPE
    loads = [
        pltpu.make_async_copy(source, target, sems.at[k])
        for k, (source, target) in enumerate(
            [(rope_hbm, rope_ref), (nope_hbm, nope_ref), (up_hbm, up_ref)]
        )
    ]
    for copy in loads:
        copy.start()
    if fetch:
        streams = stream(weight_ref, 0, stage_ref, stream_sems)
        for copy in streams:
            copy.start()
    shape = cos_ref.shape
    position = offset_ref[0] + lax.broadcasted_iota(jnp.int32, shape, 1)
    index = lax.broadcasted_iota(jnp.int32, shape, 0).astype(jnp.float32)
    frequency = jnp.exp(index * (-2.0 * math.log(10000.0) / ROPE))
    angle = position.astype(jnp.float32) * frequency
    cos_ref[...] = jnp.cos(angle)
    sin_ref[...] = jnp.sin(angle)
    mine = pl.ds(pl.multiple_of(lax.axis_index("ctx") * tokens, LANES), tokens)
    cosine = cos_ref[:, mine]
    sine = sin_ref[:, mine]
    turn_ref[...] = jnp.concatenate([cosine, cosine, -sine, sine], 0).T
    for copy in loads:
        copy.wait()

    @pl.loop(0, heads // pair)
    def _(group):
        nope_at = pl.multiple_of(group * pair * NOPE, LANES)
        rope_at = pl.multiple_of(group * pair * ROPE, LANES)
        ropes = rope_ref[:, pl.ds(rope_at, pair * ROPE)].astype(jnp.float32)
        nopes = nope_ref[:, pl.ds(nope_at, pair * NOPE)]
        for head in range(pair):
            nope = nopes[:, head * NOPE : (head + 1) * NOPE]
            latent = jnp.dot(
                nope, up_ref[group * pair + head], preferred_element_type=jnp.float32
            )
            out_ref[group * pair + head, :, :LATENT] = (latent * SCALE).astype(jnp.bfloat16)
            raw = ropes[:, head * ROPE : (head + 1) * ROPE]
            swapped = jnp.concatenate([raw[:, HALF:], raw[:, :HALF]], 1)
            turned = raw * turn_ref[:, :ROPE] + swapped * turn_ref[:, ROPE:]
            pad = jnp.zeros((tokens, WIDE - ENTRIES), jnp.float32)
            filled = jnp.concatenate([turned * SCALE, pad], 1)
            out_ref[group * pair + head, :, LATENT:] = filled.astype(jnp.bfloat16)

    if fetch:
        for copy in streams:
            copy.wait()


def front(ctx_size, offset, q_nope, q_rope, up_key, weight):
    tokens = q_nope.shape[0]
    heads = up_key.shape[0]
    vmem = pl.BlockSpec(memory_space=pltpu.VMEM)
    hbm = pl.BlockSpec(memory_space=pltpu.HBM)
    table = pltpu.VMEM((HALF, ctx_size * tokens), jnp.float32)
    in_specs = [pl.BlockSpec(memory_space=pltpu.SMEM), hbm, hbm, hbm]
    out_shape = [pltpu.VMEM((heads, tokens, WIDE), jnp.bfloat16), table, table]
    scratch = [
        pltpu.VMEM(q_nope.shape, q_nope.dtype),
        pltpu.VMEM(q_rope.shape, q_rope.dtype),
        pltpu.VMEM(up_key.shape, up_key.dtype),
        pltpu.VMEM((tokens, 2 * ROPE), jnp.float32),
        pltpu.SemaphoreType.DMA((3,)),
    ]
    args = [offset, q_nope, q_rope, up_key]
    if weight is not None:
        in_specs.append(hbm)
        out_shape.append(pltpu.VMEM(weight[1], weight[0].dtype))
        scratch.append(pltpu.SemaphoreType.DMA((STREAMS,)))
        args.append(weight[0])
    return pl.pallas_call(
        functools.partial(front_kernel, weight is not None),
        in_specs=in_specs,
        out_specs=[vmem] * len(out_shape),
        out_shape=out_shape,
        scratch_shapes=scratch,
        name="front",
        compiler_params=pltpu.CompilerParams(vmem_limit_bytes=8 * MIB),
        cost_estimate=pl.CostEstimate(
            flops=2 * heads * tokens * NOPE * LATENT, bytes_accessed=36 * MIB, transcendentals=0
        ),
    )(args[0], *in_hbm(*args[1:]))


def attend_kernel(step, first, counts_ref, q_ref, mine_ref, theirs_ref, cache_ref, group_ref, *refs):
    if first is None:
        cos_ref, sin_ref, up_ref, out_ref, keys_ref, bias_ref, cached_ref = refs
    else:
        cos_ref, sin_ref, up_ref, weight_ref, out_ref, stage_ref, *refs = refs
        keys_ref, bias_ref, cached_ref, sems = refs
        streams = stream(weight_ref, first, stage_ref, sems)
        for copy in streams:
            copy.start()
    shifts = mine_ref.shape[0]
    size = shifts + 1
    slots, tokens = cache_ref.shape[0], group_ref.shape[1]
    features = ENTRIES // 2
    tiles = WIDE // LANES
    ctx = lax.axis_index("ctx")
    core = lax.axis_index("tp") % 2
    keys_ref[ENTRIES:] = jnp.zeros((WIDE - ENTRIES, keys_ref.shape[1]), jnp.bfloat16)
    cached_ref[:slots, :ENTRIES] = cache_ref[...].astype(jnp.float32)
    cached_ref[:, ENTRIES:] = jnp.zeros((size * slots, WIDE - ENTRIES), jnp.float32)
    keys_ref[:ENTRIES, :tokens] = group_ref[...]
    for shift in range(shifts):
        lanes = slice((shift + 1) * tokens, (shift + 2) * tokens)
        for side, part in ((core, mine_ref), (1 - core, theirs_ref)):
            start = pl.multiple_of(side * features, 16)
            keys_ref[pl.ds(start, features), lanes] = part[shift, :features]
            start = pl.multiple_of((shift + 1) * slots + side * (slots // 2), 16)
            for tile in range(tiles):
                base = features + tile * (slots // 2)
                piece = part[shift, base : base + slots // 2].astype(jnp.float32)
                cached_ref[pl.ds(start, slots // 2), tile * LANES : (tile + 1) * LANES] = piece
    row = lax.broadcasted_iota(jnp.int32, (tokens, tokens), 0)
    lane = lax.broadcasted_iota(jnp.int32, (tokens, tokens), 1)
    bias_ref[:, :tokens] = jnp.where(lane <= row, 0.0, HIDDEN)
    slot = lax.broadcasted_iota(jnp.int32, (tokens, size * slots), 1)
    limit = jnp.full(slot.shape, counts_ref[ctx], jnp.int32)
    for shift in range(size):
        owner = lax.rem(ctx - shift + size, size)
        lanes = slice(shift * tokens, (shift + 1) * tokens)
        if shift > 0:
            shown = jnp.where(owner < ctx, 0.0, HIDDEN)
            bias_ref[:, lanes] = jnp.full((tokens, tokens), shown, jnp.float32)
            limit = jnp.where(slot >= shift * slots, shift * slots + counts_ref[owner], limit)
        where = pl.ds(pl.multiple_of(owner * tokens, LANES), tokens)
        cosine = cos_ref[:, where]
        sine = sin_ref[:, where]
        ahead = keys_ref[LATENT : LATENT + HALF, lanes].astype(jnp.float32)
        behind = keys_ref[LATENT + HALF : ENTRIES, lanes].astype(jnp.float32)
        keys_ref[LATENT : LATENT + HALF, lanes] = (ahead * cosine - behind * sine).astype(
            jnp.bfloat16
        )
        keys_ref[LATENT + HALF : ENTRIES, lanes] = (behind * cosine + ahead * sine).astype(
            jnp.bfloat16
        )
    bias_ref[:, size * tokens :] = jnp.where(slot < limit, 0.0, HIDDEN)
    keys_ref[:, size * tokens :] = cached_ref[...].T.astype(jnp.bfloat16)

    width = q_ref.shape[2]

    @pl.loop(0, q_ref.shape[0] // step)
    def _(group):
        queries = q_ref[pl.ds(group * step, step)].reshape(step * tokens, width)
        tail = size * tokens
        scores = jnp.concatenate(
            [
                jnp.dot(queries, keys_ref[:, :tail], preferred_element_type=jnp.float32),
                jnp.dot(queries, keys_ref[:, tail:], preferred_element_type=jnp.float32),
            ],
            1,
        )
        scores = scores.reshape(step, tokens, -1) + bias_ref[...][None]
        peak = jnp.max(scores, axis=2, keepdims=True)
        expos = jnp.exp2(scores - peak)
        total = jnp.sum(expos, axis=2, keepdims=True)
        weights = expos.astype(jnp.bfloat16).reshape(step * tokens, -1)
        mixed = lax.dot_general(
            weights, keys_ref[:LATENT], (((1,), (1,)), ((), ())), preferred_element_type=jnp.float32
        )
        attended = (mixed.reshape(step, tokens, LATENT) / total).astype(jnp.bfloat16)
        values = [
            jnp.dot(attended[head], up_ref[group * step + head], preferred_element_type=jnp.float32)
            for head in range(step)
        ]
        lanes = pl.ds(pl.multiple_of(group * step * VDIM, LANES), step * VDIM)
        out_ref[:, lanes] = jnp.concatenate(values, 1).astype(jnp.bfloat16)

    if first is not None:
        for copy in streams:
            copy.wait()


def attend(counts, queries, mine, theirs, cache, group_t, cosine, sine, up_value, weight, base):
    heads, tokens, width = queries.shape
    size = mine.shape[0] + 1
    slots = cache.shape[0]
    total = size * (tokens + slots)
    step = heads
    while step > 1 and step * tokens * total * 4 > 3 * MIB:
        step //= 2
    vmem = pl.BlockSpec(memory_space=pltpu.VMEM)
    in_specs = [pl.BlockSpec(memory_space=pltpu.SMEM)] + [vmem] * 8
    out_shape = [pltpu.VMEM((tokens, heads * VDIM), jnp.bfloat16)]
    scratch = [
        pltpu.VMEM((WIDE, total), jnp.bfloat16),
        pltpu.VMEM((tokens, total), jnp.float32),
        pltpu.VMEM((size * slots, WIDE), jnp.float32),
    ]
    args = [counts, queries, mine, theirs, cache, group_t, cosine, sine, up_value]
    if base is not None:
        in_specs.append(pl.BlockSpec(memory_space=pltpu.HBM))
        out_shape.append(pltpu.VMEM((weight.shape[0] - base, weight.shape[1]), weight.dtype))
        scratch.append(pltpu.SemaphoreType.DMA((STREAMS,)))
        args += in_hbm(weight)
    return pl.pallas_call(
        functools.partial(attend_kernel, step, base),
        in_specs=in_specs,
        out_specs=[vmem] * len(out_shape),
        out_shape=out_shape,
        scratch_shapes=scratch,
        name="attend",
        compiler_params=pltpu.CompilerParams(vmem_limit_bytes=10 * MIB + total * 8192),
        cost_estimate=pl.CostEstimate(
            flops=2 * heads * tokens * total * (LATENT + width),
            bytes_accessed=8 * MIB,
            transcendentals=heads * tokens * total,
        ),
    )(*args)


def project_kernel(width, deltas, theirs, add, parts, head_ref, upper_ref, lower_ref, *refs):
    tp = lax.axis_index("tp")
    side = 1 - tp % 2 if theirs else tp % 2
    split = upper_ref.shape[0]
    outs = refs[len(deltas) if add else 0 :]
    for place, delta in enumerate(deltas):
        start = pl.multiple_of((((tp // 2) ^ delta) * 2 + side) * width, LANES)
        lanes = pl.ds(start, width)
        block = jnp.dot(
            head_ref[:, :split], upper_ref[:, lanes], preferred_element_type=jnp.float32
        ) + jnp.dot(head_ref[:, split:], lower_ref[:, lanes], preferred_element_type=jnp.float32)
        if add:
            block = block + refs[place][...].astype(jnp.float32)
        block = block.astype(jnp.bfloat16)
        rows = block.shape[0] // parts
        for part in range(parts):
            outs[place * parts + part][...] = block[part * rows : (part + 1) * rows]


def project(head_out, upper, lower, width, deltas, theirs, arrived=(), parts=1):
    tokens, depth = head_out.shape
    out = jax.ShapeDtypeStruct((tokens // parts, width), jnp.bfloat16)
    count = len(deltas) * parts
    return pl.pallas_call(
        functools.partial(project_kernel, width, deltas, theirs, bool(arrived), parts),
        in_specs=[pl.BlockSpec(memory_space=pltpu.VMEM)] * (3 + len(arrived)),
        out_specs=[pl.BlockSpec(memory_space=pltpu.VMEM)] * count,
        out_shape=[out] * count,
        name="project",
        compiler_params=pltpu.CompilerParams(vmem_limit_bytes=6 * MIB),
        cost_estimate=pl.CostEstimate(
            flops=2 * len(deltas) * tokens * depth * width,
            bytes_accessed=2 * len(deltas) * tokens * width,
            transcendentals=0,
        ),
    )(head_out, upper, lower, *arrived)


def layer(
    ctx_size, tp_size, q_nope, q_rope, cache_latent, group_latent, offset, counts, up_key, up_value,
    out_weight,
):
    width = out_weight.shape[1] // tp_size
    chips = tp_size // 2
    direct = width % LANES == 0 and chips == 4
    swap = [(i, i ^ 1) for i in range(tp_size)]

    group_t = group_latent.T
    part = pack(group_t, cache_latent)
    arrived = []
    for shift in range(1, ctx_size):
        ring = [(i, (i + shift) % ctx_size) for i in range(ctx_size)]
        arrived.append(lax.ppermute(part, "ctx", ring))
    mine = jnp.stack(arrived)
    theirs = lax.ppermute(mine, "tp", swap)
    depth, columns = out_weight.shape
    base = depth // 2 if direct else None
    weight = (out_weight, (base, columns)) if direct else None
    queries, cosine, sine, *upper = front(ctx_size, offset, q_nope, q_rope, up_key, weight)
    head_out, *lower = attend(
        counts, queries, mine, theirs, cache_latent, group_t, cosine, sine, up_value, out_weight,
        base,
    )
    if not direct:
        partial = jnp.dot(head_out, out_weight, preferred_element_type=jnp.float32)
        summed = lax.psum_scatter(
            partial.astype(jnp.bfloat16), "tp", scatter_dimension=1, tiled=True
        )
        return summed.astype(jnp.bfloat16)

    def move(block, delta):
        return lax.ppermute(block, "tp", [(i, i ^ delta) for i in range(tp_size)])

    def plus(first, second):
        return (first.astype(jnp.float32) + second.astype(jnp.float32)).astype(jnp.bfloat16)

    run = functools.partial(project, upper=upper[0], lower=lower[0], width=width)
    far = [move(block, 1) for block in run(head_out, deltas=[3], theirs=True)]
    near = [move(block, 1) for block in run(head_out, deltas=[1, 2], theirs=True)]
    far_top, far_low = run(head_out, deltas=[3], theirs=False, arrived=far, parts=2)
    via_first = move(far_top, 2)
    via_second = move(far_low, 4)
    first_top, first_low, second_top, second_low = run(
        head_out, deltas=[1, 2], theirs=False, arrived=near, parts=2
    )
    got_first_top = move(first_top, 2)
    got_second_low = move(second_low, 4)
    later, first_low, second_top = lax.optimization_barrier((head_out, first_low, second_top))
    own = [move(block, 1) for block in run(later, deltas=[0], theirs=True)]
    got_first_low = move(plus(first_low, via_second), 2)
    got_second_top = move(plus(second_top, via_first), 4)
    own_top, own_low = run(later, deltas=[0], theirs=False, arrived=own, parts=2)
    halves = [(own_top, got_first_top, got_second_top), (own_low, got_first_low, got_second_low)]
    summed = [sum(block.astype(jnp.float32) for block in half) for half in halves]
    return jnp.concatenate(summed, 0).astype(jnp.bfloat16)


def solution(mesh):
    return jax.shard_map(
        functools.partial(layer, mesh.shape["ctx"], mesh.shape["tp"]),
        mesh=mesh,
        in_specs=(
            P("ctx", "tp"),
            P("ctx", "tp"),
            P("ctx", None),
            P("ctx", None),
            P(),
            P(),
            P("tp", None, None),
            P("tp", None, None),
            P("tp", None),
        ),
        out_specs=P("ctx", "tp"),
        check_vma=False,
    )
```
